32 devices in a mesh: section: 2 (over x), expert: 4 (over y, core), dp: 4 (over z).
Axes of the slice: x: 2, y: 2, z: 4, core: 2. Of those that a mesh axis runs over, the one named last changes fastest.
Arguments:
- inputs: bfloat16 [4, 512, 3072], P(None, ('expert', 'dp')), may hold values from -6 to 6
- upstream: bfloat16 [4, 512, 3072], P(None, ('expert', 'dp')), may hold values from -1.5 to 1.5
- route_mask: int32 [2, 4, 512], P('section', None, ('expert', 'dp')), may hold values from 0 to 1, as said below
- route_weights: float32 [2, 4, 512], P('section', None, ('expert', 'dp')), may hold values from 0.2 to 1
- gate_weight: bfloat16 [2, 3072, 8192], P('section', None, ('expert', 'dp')), may hold values from -0.109375 to 0.109375
- up_weight: bfloat16 [2, 3072, 8192], P('section', None, ('expert', 'dp')), may hold values from -0.109375 to 0.109375
- down_weight: bfloat16 [2, 8192, 3072], P('section', ('expert', 'dp')), may hold values from -0.0625 to 0.0625
Outputs:
- gate_grad: bfloat16 [2, 3072, 8192], P('section', None, ('expert', 'dp'))
- up_grad: bfloat16 [2, 3072, 8192], P('section', None, ('expert', 'dp'))
- down_grad: bfloat16 [2, 8192, 3072], P('section', ('expert', 'dp'))
The draws below stay inside these ranges and needn't reach their ends.
Inputs may be any that keep to these rules, and one draw needn't show every extreme that they name: `route_mask`: in each layer and micro-batch, each aligned block of 32 tokens (the tokens of one device) has at most 8 ones, and some block exactly 8.
All inputs are finite; a program needn't handle non-finite values.
Results may differ from the reference program's by a relative error of at most 0.0095.
Values may be sent and summed in bfloat16 or wider, within the bound.
A program may use at most 128 MiB of HBM per device.

```python
import jax
import jax.numpy as jnp
from jax import lax

D = 3072
H = 8192
MICRO = 4
T_DEV = 32
CAP = 8
TOKENS = 512
SECTIONS = 2
N_EXPERT = 4
N_DP = 4


def draw_route_mask(key, part):
    blocks = TOKENS // T_DEV
    count_key = jax.random.fold_in(key, 11)
    top_key = jax.random.fold_in(key, 12)
    order_key = jax.random.fold_in(key, 13)
    lowest = max(1, CAP // 3)
    counts = jax.random.randint(count_key, (SECTIONS, MICRO, blocks), lowest, CAP + 1).astype(jnp.int32)
    fullest = jax.random.randint(top_key, (SECTIONS, MICRO, 1), 0, blocks).astype(jnp.int32)
    counts = jnp.where(jnp.arange(blocks, dtype=jnp.int32)[None, None, :] == fullest, CAP, counts).astype(jnp.int32)
    scores = jax.random.randint(order_key, (SECTIONS, MICRO, blocks, T_DEV), 0, 1 << 20).astype(jnp.int32)
    scores = scores * T_DEV + jnp.arange(T_DEV, dtype=jnp.int32)[None, None, None, :]
    ranks = jnp.argsort(jnp.argsort(scores, axis=-1, stable=True), axis=-1, stable=True).astype(jnp.int32)
    chosen = (ranks < counts[:, :, :, None]).astype(jnp.int32)
    return chosen.reshape(SECTIONS, MICRO, TOKENS)


def levels(stream_key, extent, split, least, largest):
    level = 1.0
    for dim, parts in split:
        heights = jax.random.uniform(jax.random.fold_in(jax.random.fold_in(stream_key, 6), dim), (parts,), jnp.float32, least / len(split), largest / len(split))
        level = level * jnp.repeat(jnp.exp(heights), extent[dim] // parts).reshape((-1,) + (1,) * (len(extent) - 1 - dim))
    return level


def gaussian(rng, extent, scale, limit, cuts=(), kind=jnp.bfloat16):
    values = jax.random.normal(rng, extent, jnp.float32) * scale
    if len(cuts) > 0:
        values = levels(rng, extent, cuts, -0.22, 0.18) * values
    return jnp.clip(values, min=-limit, max=limit).astype(kind)


def setup_inputs(seed: int = 0) -> dict:
    arg_keys = jax.random.split(jax.random.key(seed), 8)
    return {
        "inputs": gaussian(arg_keys[0], (MICRO, TOKENS, D), 1.0, 6.0, ((1, 16),)),
        "upstream": gaussian(arg_keys[1], (MICRO, TOKENS, D), 0.25, 1.5, ((1, 16),)),
        "route_mask": draw_route_mask(jax.random.fold_in(arg_keys[7], 71), 0),
        "route_weights": jnp.clip(0.2 + 0.8 * jax.random.uniform(arg_keys[3], (SECTIONS, MICRO, TOKENS), jnp.float32) ** levels(arg_keys[3], (SECTIONS, MICRO, TOKENS), ((0, 2), (2, 16)), -0.2, 0.2), 0.2, 1.0),
        "gate_weight": gaussian(arg_keys[4], (SECTIONS, D, H), D ** -0.5, 0.109375, ((0, 2), (2, 16))),
        "up_weight": gaussian(arg_keys[5], (SECTIONS, D, H), D ** -0.5, 0.109375, ((0, 2), (2, 16))),
        "down_weight": gaussian(arg_keys[6], (SECTIONS, H, D), H ** -0.5, 0.0625, ((0, 2), (1, 16))),
    }


EPSILON = 1e-05

def normalize(layer_input):
    input_f = layer_input.astype(jnp.float32)
    scale = lax.rsqrt(lax.optimization_barrier(jnp.mean(input_f * input_f, axis=-1, keepdims=True)) + EPSILON)
    return (input_f, scale, (input_f * scale).astype(jnp.bfloat16))

def compact_table(mask):
    blocks = mask.reshape(-1, T_DEV).astype(jnp.int32)
    position = (jnp.cumsum(blocks, axis=1) - 1).astype(jnp.int32)
    chosen = (blocks[:, :, None] == 1) & (position[:, :, None] == jnp.arange(CAP, dtype=jnp.int32)[None, None, :])
    return chosen.astype(jnp.float32)

def compact(table, values):
    block_values = values.reshape(table.shape[0], T_DEV, -1).astype(jnp.float32)
    return jnp.einsum('btc,btd->bcd', table, block_values).reshape(-1, values.shape[-1]).astype(jnp.bfloat16)

def expand(table, rows):
    block_rows = rows.reshape(table.shape[0], CAP, -1).astype(jnp.float32)
    return jnp.einsum('btc,bcd->btd', table, block_rows).reshape(-1, rows.shape[-1])

def section_forward(layer_input, mask, weight, gate_w, up_w, down_w):
    shards = N_EXPERT * N_DP
    input_f, scale, normed = normalize(layer_input)
    table = compact_table(mask)
    rows = compact(table, normed)
    gate_pre = jnp.dot(rows, gate_w, preferred_element_type=jnp.float32)
    up_pre = jnp.dot(rows, up_w, preferred_element_type=jnp.float32)
    hidden = (jax.nn.silu(gate_pre) * up_pre).astype(jnp.bfloat16)
    width = hidden.shape[1] // shards
    summed = jnp.zeros((rows.shape[0], down_w.shape[1]), jnp.float32)
    for group in range(shards):
        piece = jnp.dot(hidden[:, group * width:(group + 1) * width], down_w[group * width:(group + 1) * width], preferred_element_type=jnp.float32)
        summed = summed + lax.optimization_barrier(piece.astype(jnp.bfloat16)).astype(jnp.float32)
    back = expand(table, summed.astype(jnp.bfloat16))
    return (input_f + weight[:, None] * back).astype(jnp.bfloat16)

def section_backward(layer_input, mask, weight, gate_w, up_w, down_w, flowing):
    shards = N_EXPERT * N_DP
    contract_rows = (((1,), (1,)), ((), ()))
    contract_first = (((0,), (0,)), ((), ()))
    input_f, scale, normed = normalize(layer_input)
    table = compact_table(mask)
    rows = compact(table, normed)
    flowing_f = flowing.astype(jnp.float32)
    out_grad = (weight[:, None] * flowing_f).astype(jnp.bfloat16)
    grad_rows = compact(table, out_grad)
    gate_pre = jnp.dot(rows, gate_w, preferred_element_type=jnp.float32)
    up_pre = jnp.dot(rows, up_w, preferred_element_type=jnp.float32)
    sigma = jax.nn.sigmoid(gate_pre)
    silu_val = jax.nn.silu(gate_pre)
    hidden = (silu_val * up_pre).astype(jnp.bfloat16)
    hidden_grad = lax.dot_general(grad_rows, down_w, contract_rows, preferred_element_type=jnp.float32)
    gate_pre_grad = (hidden_grad * up_pre * sigma * (1.0 + gate_pre * (1.0 - sigma))).astype(jnp.bfloat16)
    up_pre_grad = (hidden_grad * silu_val).astype(jnp.bfloat16)
    width = hidden.shape[1] // shards
    summed = jnp.zeros((rows.shape[0], gate_w.shape[0]), jnp.float32)
    for group in range(shards):
        lo_col = group * width
        hi_col = (group + 1) * width
        piece = lax.dot_general(gate_pre_grad[:, lo_col:hi_col], gate_w[:, lo_col:hi_col], contract_rows, preferred_element_type=jnp.float32) + lax.dot_general(up_pre_grad[:, lo_col:hi_col], up_w[:, lo_col:hi_col], contract_rows, preferred_element_type=jnp.float32)
        summed = summed + lax.optimization_barrier(piece.astype(jnp.bfloat16)).astype(jnp.float32)
    total = expand(table, summed.astype(jnp.bfloat16))
    inner = lax.optimization_barrier(jnp.mean(input_f * total, axis=-1, keepdims=True))
    input_grad = (flowing_f + scale * total - input_f * (scale * scale * scale) * inner).astype(jnp.bfloat16)
    gate_part = lax.dot_general(rows, gate_pre_grad, contract_first, preferred_element_type=jnp.float32)
    up_part = lax.dot_general(rows, up_pre_grad, contract_first, preferred_element_type=jnp.float32)
    down_part = lax.dot_general(hidden, grad_rows, contract_first, preferred_element_type=jnp.float32)
    return (input_grad, gate_part, up_part, down_part)

def reference(inputs, upstream, route_mask, route_weights, gate_weight, up_weight, down_weight):
    model_width = inputs.shape[-1]
    current = inputs.reshape(-1, model_width)
    saved = []
    for section_index in range(SECTIONS):
        saved.append(current)
        current = section_forward(current, route_mask[section_index], route_weights[section_index].reshape(-1), gate_weight[section_index], up_weight[section_index], down_weight[section_index])
    flowing = upstream.reshape(-1, model_width)
    gate_list = [None] * SECTIONS
    up_list = [None] * SECTIONS
    down_list = [None] * SECTIONS
    for section_index in reversed(range(SECTIONS)):
        flowing, gate_part, up_part, down_part = section_backward(saved[section_index], route_mask[section_index], route_weights[section_index].reshape(-1), gate_weight[section_index], up_weight[section_index], down_weight[section_index], flowing)
        gate_list[section_index] = gate_part
        up_list[section_index] = up_part
        down_list[section_index] = down_part
    gate_out = jnp.stack(gate_list).astype(jnp.bfloat16)
    up_out = jnp.stack(up_list).astype(jnp.bfloat16)
    down_out = jnp.stack(down_list).astype(jnp.bfloat16)
    return (gate_out, up_out, down_out)
```

```python
import jax
import jax.numpy as jnp
from jax import lax
from jax.sharding import PartitionSpec as P

CAP = 8

EPSILON = 1e-05

GROUP = ("expert", "dp")


def slot_tables(mask):
    position = jnp.cumsum(mask, axis=1) - 1
    chosen = (mask[:, :, None] == 1) & (
        position[:, :, None] == jnp.arange(CAP, dtype=jnp.int32)[None, None, :]
    )
    return chosen.astype(jnp.bfloat16)


def pick(table, values):
    return lax.dot_general(
        table, values, (((1,), (1,)), ((0,), (0,))), preferred_element_type=jnp.float32
    ).astype(values.dtype)


def place(table, mask, rows, values):
    spread = lax.dot_general(
        table, rows, (((2,), (1,)), ((0,), (0,))), preferred_element_type=jnp.float32
    ).astype(values.dtype)
    return jnp.where(mask[:, :, None] == 1, spread, values)


def row_scale(rows_f):
    return lax.rsqrt(jnp.mean(rows_f * rows_f, axis=-1, keepdims=True) + EPSILON)


def gather(block):
    flat = block.reshape(-1, block.shape[-1])
    return lax.all_gather(flat, GROUP, axis=0, tiled=True)


def scatter_sum(partial, like):
    summed = lax.psum_scatter(partial, GROUP, scatter_dimension=0, tiled=True)
    return summed.reshape(like.shape)


def mm(a, b, dims=((1,), (0,))):
    return lax.dot_general(a, b, (dims, ((), ())), preferred_element_type=jnp.float32)


def shards(inputs, upstream, route_mask, route_weights, gate_weight, up_weight, down_weight):
    sections = lax.axis_size("section")
    section = lax.axis_index("section")
    gate_w, up_w, down_w = gate_weight[0], up_weight[0], down_weight[0]
    mask = route_mask[0]
    table = slot_tables(mask)
    weights = jnp.sum(table.astype(jnp.float32) * route_weights[0][:, :, None], axis=1)[:, :, None]
    up_route = [(i, i + 1) for i in range(sections - 1)]
    down_route = [(i + 1, i) for i in range(sections - 1)]
    next_table = lax.ppermute(table, "section", down_route)
    previous_table = lax.ppermute(table, "section", up_route)

    def activations(gate_pre, up_pre):
        return (jax.nn.silu(gate_pre) * up_pre).astype(jnp.bfloat16)

    def out_grad(g_rows):
        return (weights * g_rows.astype(jnp.float32)).astype(jnp.bfloat16)

    stream = inputs
    current = pick(table, inputs)
    last_rows = pick(table, upstream)
    grads_in = last_rows
    first_grad = out_grad(last_rows)
    is_last = section == sections - 1
    own = current
    all_rows = gate_pre = up_pre = all_grads = hidden_grad = None
    for t in range(sections):
        active = section == t
        own = jnp.where(active, current, own)
        own_f = current.astype(jnp.float32)
        normed = (own_f * row_scale(own_f)).astype(jnp.bfloat16)
        send = jnp.where(is_last, first_grad, normed) if t == 0 and sections > 1 else normed
        got = gather(send)
        if t == 0:
            all_grads = got if sections > 1 else gather(first_grad)
            hidden_grad = mm(all_grads, down_w, ((1,), (1,)))
            all_rows = got
            gate_pre = mm(got, gate_w)
            up_pre = mm(got, up_w)
            new_gate, new_up = gate_pre, up_pre
        else:
            new_gate, new_up = mm(got, gate_w), mm(got, up_w)
            all_rows = jnp.where(active, got, all_rows)
            gate_pre = jnp.where(active, new_gate, gate_pre)
            up_pre = jnp.where(active, new_up, up_pre)
        if t < sections - 1:
            partial = mm(activations(new_gate, new_up), down_w).astype(jnp.bfloat16)
            back = scatter_sum(partial, current).astype(jnp.float32)
            output_rows = (own_f + weights * back).astype(jnp.bfloat16)
            output = place(table, mask, output_rows, stream)
            if t == sections - 2:
                current = lax.ppermute(pick(next_table, output), "section", up_route)
            else:
                stream = lax.ppermute(output, "section", up_route)
                current = pick(table, stream)

    sigma = jax.nn.sigmoid(gate_pre)
    silu_val = jax.nn.silu(gate_pre)
    hidden = activations(gate_pre, up_pre)
    slope = up_pre * sigma * (1.0 + gate_pre * (1.0 - sigma))
    own_f = own.astype(jnp.float32)
    scale = row_scale(own_f)

    flow = upstream
    for t in reversed(range(sections)):
        active = section == t
        if t < sections - 1:
            got = gather(out_grad(grads_in))
            all_grads = jnp.where(active, got, all_grads)
            hidden_grad = mm(all_grads, down_w, ((1,), (1,)))
        gate_units = (hidden_grad * slope).astype(jnp.bfloat16)
        up_units = (hidden_grad * silu_val).astype(jnp.bfloat16)
        if t > 0:
            partial = mm(gate_units, gate_w, ((1,), (1,))) + mm(up_units, up_w, ((1,), (1,)))
            total = scatter_sum(partial.astype(jnp.bfloat16), own).astype(jnp.float32)
            inner = jnp.mean(own_f * total, axis=-1, keepdims=True)
            grad_rows = (
                grads_in.astype(jnp.float32)
                + scale * total
                - own_f * (scale * scale * scale) * inner
            ).astype(jnp.bfloat16)
            result = place(table, mask, grad_rows, flow)
            if t == 1:
                grads_in = lax.ppermute(pick(previous_table, result), "section", down_route)
            else:
                flow = lax.ppermute(result, "section", down_route)
                grads_in = pick(table, flow)

    gate_grad = mm(all_rows, gate_units, ((0,), (0,)))
    up_grad = mm(all_rows, up_units, ((0,), (0,)))
    down_grad = mm(hidden, all_grads, ((0,), (0,)))
    return (
        gate_grad.astype(jnp.bfloat16)[None],
        up_grad.astype(jnp.bfloat16)[None],
        down_grad.astype(jnp.bfloat16)[None],
    )


def solution(mesh):
    return jax.shard_map(
        shards,
        mesh=mesh,
        in_specs=(
            P(None, ("expert", "dp"), None),
            P(None, ("expert", "dp"), None),
            P("section", None, ("expert", "dp")),
            P("section", None, ("expert", "dp")),
            P("section", None, ("expert", "dp")),
            P("section", None, ("expert", "dp")),
            P("section", ("expert", "dp"), None),
        ),
        out_specs=(
            P("section", None, ("expert", "dp")),
            P("section", None, ("expert", "dp")),
            P("section", ("expert", "dp"), None),
        ),
        check_vma=False,
    )
```

```python
import jax
import jax.numpy as jnp
from jax import lax
from jax.experimental import pallas as pl
from jax.experimental.pallas import tpu as pltpu
from jax.sharding import PartitionSpec as P

CAP = 8

EPSILON = 1e-05

GROUP = ("expert", "dp")


def slot_tables(mask):
    position = jnp.cumsum(mask, axis=1) - 1
    chosen = (mask[:, :, None] == 1) & (
        position[:, :, None] == jnp.arange(CAP, dtype=jnp.int32)[None, None, :]
    )
    return chosen.astype(jnp.bfloat16)


def pick(table, values):
    return lax.dot_general(
        table, values, (((1,), (1,)), ((0,), (0,))), preferred_element_type=jnp.float32
    ).astype(values.dtype)


def place(table, mask, rows, values):
    spread = lax.dot_general(
        table, rows, (((2,), (1,)), ((0,), (0,))), preferred_element_type=jnp.float32
    ).astype(values.dtype)
    return jnp.where(mask[:, :, None] == 1, spread, values)


def row_scale(rows_f):
    return lax.rsqrt(jnp.mean(rows_f * rows_f, axis=-1, keepdims=True) + EPSILON)


SIDE = 4


def neighbours():
    e, z = lax.axis_index("expert"), lax.axis_index("dp")
    mate = e + 1 - 2 * lax.rem(e, 2)
    across = lax.rem(e + 2, SIDE)
    return e, z, mate, across


def remote(src, dst, send_sem, recv_sem, target):
    return pltpu.make_async_remote_copy(
        src_ref=src,
        dst_ref=dst,
        send_sem=send_sem,
        recv_sem=recv_sem,
        device_id=target,
        device_id_type=pl.DeviceIdType.MESH,
    )


def entry_barrier(z, mate, across):
    barrier = pltpu.get_barrier_semaphore()

    def greet(target):
        pl.semaphore_signal(
            barrier, inc=1, device_id=target, device_id_type=pl.DeviceIdType.MESH
        )

    greet({"expert": mate})
    greet({"expert": across})

    @pl.when(z > 0)
    def _():
        greet({"dp": z - 1})

    @pl.when(z < SIDE - 1)
    def _():
        greet({"dp": z + 1})

    @pl.when((z > 0) & (z < SIDE - 1))
    def _():
        pl.semaphore_wait(barrier, 4)

    @pl.when((z == 0) | (z == SIDE - 1))
    def _():
        pl.semaphore_wait(barrier, 3)


def gather_kernel(x_ref, out_ref, local_sem, send_sem, recv_sem):
    e, z, mate, across = neighbours()
    entry_barrier(z, mate, across)

    def route(slot, kind, target, src=None):
        block = out_ref.at[slot] if src is None else src
        return remote(
            block, out_ref.at[slot], send_sem.at[slot, kind], recv_sem.at[slot], target
        )

    def up(slot, src=None):
        return route(slot, 0, {"dp": z + 1}, src)

    def down(slot, src=None):
        return route(slot, 1, {"dp": z - 1}, src)

    def over(slot, src=None):
        return route(slot, 2, {"expert": across}, src)

    def core(slot, src=None):
        return route(slot, 3, {"expert": mate}, src)

    mine = e * SIDE + z

    def own_sends(act):
        @pl.when(z < SIDE - 1)
        def _():
            act(up(mine, x_ref))

        @pl.when(z > 0)
        def _():
            act(down(mine, x_ref))

        act(over(mine, x_ref))
        act(core(mine, x_ref))

    keep = pltpu.make_async_copy(x_ref, out_ref.at[mine], local_sem)
    own_sends(lambda copy: copy.start())
    keep.start()

    def chain(act, arrive):
        for d in range(1, SIDE):

            @pl.when(z - d >= 0)
            def _():
                slot = e * SIDE + z - d
                if arrive:
                    core(slot).wait_recv()

                @pl.when(z < SIDE - 1)
                def _():
                    act(up(slot))

                act(over(slot))
                act(core(slot))

            @pl.when(z + d < SIDE)
            def _():
                slot = e * SIDE + z + d
                if arrive:
                    core(slot).wait_recv()

                @pl.when(z > 0)
                def _():
                    act(down(slot))

                act(over(slot))
                act(core(slot))

    chain(lambda copy: copy.start(), True)
    for d in range(SIDE):
        slot = across * SIDE + lax.rem(z + d, SIDE)
        core(slot).wait_recv()
        core(slot).start()
    far = lax.rem(mate + 2, SIDE)
    for d in range(SIDE):
        core(mate * SIDE + lax.rem(z + d, SIDE)).wait_recv()
        core(far * SIDE + lax.rem(z + d, SIDE)).wait_recv()
    own_sends(lambda copy: copy.wait_send())
    keep.wait()
    chain(lambda copy: copy.wait_send(), False)
    for d in range(SIDE):
        core(across * SIDE + lax.rem(z + d, SIDE)).wait_send()


def scatter_kernel(
    x_ref, out_ref, core_in, over_in, up_in, down_in, over_out, chain_out,
    core_s, core_r, over_s, over_r, up_s, up_r, down_s, down_r,
):
    e, z, mate, across = neighbours()
    far = lax.rem(mate + 2, SIDE)
    entry_barrier(z, mate, across)
    order = [lax.rem(z + d, SIDE) for d in (2, 3, 1, 0)]

    def f32(block):
        return block.astype(jnp.float32)

    def core(half, q):
        owner = far if half == 0 else mate
        return remote(
            x_ref.at[owner * SIDE + q], core_in.at[half * SIDE + q],
            core_s.at[half * SIDE + q], core_r.at[half * SIDE + q], {"expert": mate},
        )

    def over(q):
        return remote(
            over_out.at[q], over_in.at[q], over_s.at[q], over_r.at[q], {"expert": across}
        )

    def up(q):
        return remote(chain_out.at[q], up_in.at[q], up_s.at[q], up_r.at[q], {"dp": z + 1})

    def down(q):
        return remote(
            chain_out.at[q], down_in.at[q], down_s.at[q], down_r.at[q], {"dp": z - 1}
        )

    for half in range(2):
        for q in order:
            core(half, q).start()
    for q in order:
        core(0, q).wait_recv()
        both = f32(x_ref[across * SIDE + q]) + f32(core_in[q])
        over_out[q] = both.astype(jnp.bfloat16)
        over(q).start()
    for q in order[:-1]:
        core(1, q).wait_recv()
        over(q).wait_recv()
        both = f32(x_ref[e * SIDE + q]) + f32(core_in[SIDE + q]) + f32(over_in[q])
        chain_out[q] = both.astype(jnp.bfloat16)

        @pl.when(q > z)
        def _():
            @pl.when(z > 0)
            def _():
                up(q).wait_recv()
                chain_out[q] = (f32(chain_out[q]) + f32(up_in[q])).astype(jnp.bfloat16)

            up(q).start()

        @pl.when(q < z)
        def _():
            @pl.when(z < SIDE - 1)
            def _():
                down(q).wait_recv()
                chain_out[q] = (f32(chain_out[q]) + f32(down_in[q])).astype(jnp.bfloat16)

            down(q).start()

    core(1, z).wait_recv()
    over(z).wait_recv()
    total = f32(x_ref[e * SIDE + z]) + f32(core_in[SIDE + z]) + f32(over_in[z])

    @pl.when(z == 0)
    def _():
        down(z).wait_recv()
        out_ref[...] = (total + f32(down_in[z])).astype(jnp.bfloat16)

    @pl.when(z == SIDE - 1)
    def _():
        up(z).wait_recv()
        out_ref[...] = (total + f32(up_in[z])).astype(jnp.bfloat16)

    @pl.when((z > 0) & (z < SIDE - 1))
    def _():
        up(z).wait_recv()
        down(z).wait_recv()
        out_ref[...] = (total + f32(up_in[z]) + f32(down_in[z])).astype(jnp.bfloat16)

    for half in range(2):
        for q in order:
            core(half, q).wait_send()
    for q in order:
        over(q).wait_send()
    for q in order[:-1]:

        @pl.when(q > z)
        def _():
            up(q).wait_send()

        @pl.when(q < z)
        def _():
            down(q).wait_send()


def square_group():
    return lax.axis_size("expert") == SIDE and lax.axis_size("dp") == SIDE


def gather(block):
    flat = block.reshape(-1, block.shape[-1])
    if not square_group():
        return lax.all_gather(flat, GROUP, axis=0, tiled=True)
    slots = SIDE * SIDE
    got = pl.pallas_call(
        gather_kernel,
        out_shape=jax.ShapeDtypeStruct((slots,) + flat.shape, flat.dtype),
        in_specs=[pl.BlockSpec(memory_space=pl.ANY)],
        out_specs=pl.BlockSpec(memory_space=pl.ANY),
        scratch_shapes=[
            pltpu.SemaphoreType.DMA,
            pltpu.SemaphoreType.DMA((slots, 4)),
            pltpu.SemaphoreType.DMA((slots,)),
        ],
        compiler_params=pltpu.CompilerParams(collective_id=0, has_side_effects=True),
    )(flat)
    return got.reshape(-1, flat.shape[-1])


def scatter_sum(partial, like):
    if not square_group():
        summed = lax.psum_scatter(partial, GROUP, scatter_dimension=0, tiled=True)
        return summed.reshape(like.shape)
    width = partial.shape[-1]
    rows = partial.shape[0] // (SIDE * SIDE)
    buffers = [pltpu.VMEM((n, rows, width), partial.dtype) for n in (8, 4, 4, 4, 4, 4)]
    sems = [pltpu.SemaphoreType.DMA((n,)) for n in (8, 8, 4, 4, 4, 4, 4, 4)]
    summed = pl.pallas_call(
        scatter_kernel,
        out_shape=jax.ShapeDtypeStruct((rows, width), partial.dtype),
        in_specs=[pl.BlockSpec(memory_space=pltpu.VMEM)],
        out_specs=pl.BlockSpec(memory_space=pltpu.VMEM),
        scratch_shapes=buffers + sems,
        compiler_params=pltpu.CompilerParams(
            collective_id=1, has_side_effects=True, vmem_limit_bytes=32 * 1024 * 1024
        ),
    )(partial.reshape(SIDE * SIDE, rows, width))
    return summed.reshape(like.shape)


def mm(a, b, dims=((1,), (0,))):
    return lax.dot_general(a, b, (dims, ((), ())), preferred_element_type=jnp.float32)


def shards(inputs, upstream, route_mask, route_weights, gate_weight, up_weight, down_weight):
    sections = lax.axis_size("section")
    section = lax.axis_index("section")
    gate_w, up_w, down_w = gate_weight[0], up_weight[0], down_weight[0]
    mask = route_mask[0]
    table = slot_tables(mask)
    weights = jnp.sum(table.astype(jnp.float32) * route_weights[0][:, :, None], axis=1)[:, :, None]
    up_route = [(i, i + 1) for i in range(sections - 1)]
    down_route = [(i + 1, i) for i in range(sections - 1)]
    next_table = lax.ppermute(table, "section", down_route)
    previous_table = lax.ppermute(table, "section", up_route)

    def activations(gate_pre, up_pre):
        return (jax.nn.silu(gate_pre) * up_pre).astype(jnp.bfloat16)

    def out_grad(g_rows):
        return (weights * g_rows.astype(jnp.float32)).astype(jnp.bfloat16)

    stream = inputs
    current = pick(table, inputs)
    last_rows = pick(table, upstream)
    grads_in = last_rows
    first_grad = out_grad(last_rows)
    is_last = section == sections - 1
    own = current
    all_rows = gate_pre = up_pre = all_grads = hidden_grad = None
    for t in range(sections):
        active = section == t
        own = jnp.where(active, current, own)
        own_f = current.astype(jnp.float32)
        normed = (own_f * row_scale(own_f)).astype(jnp.bfloat16)
        send = jnp.where(is_last, first_grad, normed) if t == 0 and sections > 1 else normed
        got = gather(send)
        if t == 0:
            all_grads = got if sections > 1 else gather(first_grad)
            hidden_grad = mm(all_grads, down_w, ((1,), (1,)))
            all_rows = got
            gate_pre = mm(got, gate_w)
            up_pre = mm(got, up_w)
            new_gate, new_up = gate_pre, up_pre
        else:
            new_gate, new_up = mm(got, gate_w), mm(got, up_w)
            all_rows = jnp.where(active, got, all_rows)
            gate_pre = jnp.where(active, new_gate, gate_pre)
            up_pre = jnp.where(active, new_up, up_pre)
        if t < sections - 1:
            partial = mm(activations(new_gate, new_up), down_w).astype(jnp.bfloat16)
            back = scatter_sum(partial, current).astype(jnp.float32)
            output_rows = (own_f + weights * back).astype(jnp.bfloat16)
            output = place(table, mask, output_rows, stream)
            if t == sections - 2:
                current = lax.ppermute(pick(next_table, output), "section", up_route)
            else:
                stream = lax.ppermute(output, "section", up_route)
                current = pick(table, stream)

    sigma = jax.nn.sigmoid(gate_pre)
    silu_val = jax.nn.silu(gate_pre)
    hidden = activations(gate_pre, up_pre)
    slope = up_pre * sigma * (1.0 + gate_pre * (1.0 - sigma))
    own_f = own.astype(jnp.float32)
    scale = row_scale(own_f)

    flow = upstream
    for t in reversed(range(sections)):
        active = section == t
        if t < sections - 1:
            got = gather(out_grad(grads_in))
            all_grads = jnp.where(active, got, all_grads)
            hidden_grad = mm(all_grads, down_w, ((1,), (1,)))
        gate_units = (hidden_grad * slope).astype(jnp.bfloat16)
        up_units = (hidden_grad * silu_val).astype(jnp.bfloat16)
        if t > 0:
            partial = mm(gate_units, gate_w, ((1,), (1,))) + mm(up_units, up_w, ((1,), (1,)))
            total = scatter_sum(partial.astype(jnp.bfloat16), own).astype(jnp.float32)
            inner = jnp.mean(own_f * total, axis=-1, keepdims=True)
            grad_rows = (
                grads_in.astype(jnp.float32)
                + scale * total
                - own_f * (scale * scale * scale) * inner
            ).astype(jnp.bfloat16)
            result = place(table, mask, grad_rows, flow)
            if t == 1:
                grads_in = lax.ppermute(pick(previous_table, result), "section", down_route)
            else:
                flow = lax.ppermute(result, "section", down_route)
                grads_in = pick(table, flow)

    gate_grad = mm(all_rows, gate_units, ((0,), (0,)))
    up_grad = mm(all_rows, up_units, ((0,), (0,)))
    down_grad = mm(hidden, all_grads, ((0,), (0,)))
    return (
        gate_grad.astype(jnp.bfloat16)[None],
        up_grad.astype(jnp.bfloat16)[None],
        down_grad.astype(jnp.bfloat16)[None],
    )


def solution(mesh):
    return jax.shard_map(
        shards,
        mesh=mesh,
        in_specs=(
            P(None, ("expert", "dp"), None),
            P(None, ("expert", "dp"), None),
            P("section", None, ("expert", "dp")),
            P("section", None, ("expert", "dp")),
            P("section", None, ("expert", "dp")),
            P("section", None, ("expert", "dp")),
            P("section", ("expert", "dp"), None),
        ),
        out_specs=(
            P("section", None, ("expert", "dp")),
            P("section", None, ("expert", "dp")),
            P("section", ("expert", "dp"), None),
        ),
        check_vma=False,
    )
```

```python
import jax
import jax.numpy as jnp
from jax import lax
from jax.experimental import pallas as pl
from jax.experimental.pallas import tpu as pltpu
from jax.sharding import PartitionSpec as P

CAP = 8

EPSILON = 1e-05

GROUP = ("expert", "dp")


def slot_tables(mask):
    position = jnp.cumsum(mask, axis=1) - 1
    chosen = (mask[:, :, None] == 1) & (
        position[:, :, None] == jnp.arange(CAP, dtype=jnp.int32)[None, None, :]
    )
    return chosen.astype(jnp.bfloat16)


def pick(table, values):
    return lax.dot_general(
        table, values, (((1,), (1,)), ((0,), (0,))), preferred_element_type=jnp.float32
    ).astype(values.dtype)


def place(table, mask, rows, values):
    spread = lax.dot_general(
        table, rows, (((2,), (1,)), ((0,), (0,))), preferred_element_type=jnp.float32
    ).astype(values.dtype)
    return jnp.where(mask[:, :, None] == 1, spread, values)


def row_scale(rows_f):
    return lax.rsqrt(jnp.mean(rows_f * rows_f, axis=-1, keepdims=True) + EPSILON)


SIDE = 4
CHUNKS = 2


def neighbours():
    e, z = lax.axis_index("expert"), lax.axis_index("dp")
    mate = e + 1 - 2 * lax.rem(e, 2)
    across = lax.rem(e + 2, SIDE)
    return e, z, mate, across


def remote(src, dst, send_sem, recv_sem, target):
    return pltpu.make_async_remote_copy(
        src_ref=src,
        dst_ref=dst,
        send_sem=send_sem,
        recv_sem=recv_sem,
        device_id=target,
        device_id_type=pl.DeviceIdType.MESH,
    )


def entry_barrier(z, mate, across):
    barrier = pltpu.get_barrier_semaphore()

    def greet(target):
        pl.semaphore_signal(
            barrier, inc=1, device_id=target, device_id_type=pl.DeviceIdType.MESH
        )

    greet({"expert": mate})
    greet({"expert": across})

    @pl.when(z > 0)
    def _():
        greet({"dp": z - 1})

    @pl.when(z < SIDE - 1)
    def _():
        greet({"dp": z + 1})

    @pl.when((z > 0) & (z < SIDE - 1))
    def _():
        pl.semaphore_wait(barrier, 4)

    @pl.when((z == 0) | (z == SIDE - 1))
    def _():
        pl.semaphore_wait(barrier, 3)


def gather_kernel(x_ref, out_ref, local_sem, send_sem, recv_sem):
    e, z, mate, across = neighbours()
    entry_barrier(z, mate, across)

    def route(h, slot, kind, target, mine=False):
        block = x_ref.at[h] if mine else out_ref.at[h, slot]
        return remote(
            block, out_ref.at[h, slot], send_sem.at[h, slot, kind], recv_sem.at[h, slot], target
        )

    def up(h, slot, mine=False):
        return route(h, slot, 0, {"dp": z + 1}, mine)

    def down(h, slot, mine=False):
        return route(h, slot, 1, {"dp": z - 1}, mine)

    def over(h, slot, mine=False):
        return route(h, slot, 2, {"expert": across}, mine)

    def core(h, slot, mine=False):
        return route(h, slot, 3, {"expert": mate}, mine)

    own = e * SIDE + z

    def own_sends(act):
        for h in range(CHUNKS):

            @pl.when(z < SIDE - 1)
            def _():
                act(up(h, own, True))

            @pl.when(z > 0)
            def _():
                act(down(h, own, True))

            act(over(h, own, True))
            act(core(h, own, True))

    def keep(h):
        return pltpu.make_async_copy(x_ref.at[h], out_ref.at[h, own], local_sem.at[h])

    own_sends(lambda copy: copy.start())
    for h in range(CHUNKS):
        keep(h).start()

    def chain(act, arrive):
        for d in range(1, SIDE):
            for h in range(CHUNKS):

                @pl.when(z - d >= 0)
                def _():
                    slot = e * SIDE + z - d
                    if arrive:
                        core(h, slot).wait_recv()

                    @pl.when(z < SIDE - 1)
                    def _():
                        act(up(h, slot))

                    act(over(h, slot))
                    act(core(h, slot))

                @pl.when(z + d < SIDE)
                def _():
                    slot = e * SIDE + z + d
                    if arrive:
                        core(h, slot).wait_recv()

                    @pl.when(z > 0)
                    def _():
                        act(down(h, slot))

                    act(over(h, slot))
                    act(core(h, slot))

    chain(lambda copy: copy.start(), True)
    for d in range(SIDE):
        for h in range(CHUNKS):
            slot = across * SIDE + lax.rem(z + d, SIDE)
            core(h, slot).wait_recv()
            core(h, slot).start()
    far = lax.rem(mate + 2, SIDE)
    for h in range(CHUNKS):
        for d in range(SIDE):
            core(h, mate * SIDE + lax.rem(z + d, SIDE)).wait_recv()
            core(h, far * SIDE + lax.rem(z + d, SIDE)).wait_recv()
    own_sends(lambda copy: copy.wait_send())
    for h in range(CHUNKS):
        keep(h).wait()
    chain(lambda copy: copy.wait_send(), False)
    for h in range(CHUNKS):
        for d in range(SIDE):
            core(h, across * SIDE + lax.rem(z + d, SIDE)).wait_send()


def scatter_kernel(
    x_ref, out_ref, core_in, over_in, up_in, down_in, over_out, chain_out,
    core_s, core_r, over_s, over_r, up_s, up_r, down_s, down_r,
):
    e, z, mate, across = neighbours()
    far = lax.rem(mate + 2, SIDE)
    entry_barrier(z, mate, across)
    order = [lax.rem(z + d, SIDE) for d in (2, 3, 1, 0)]

    def f32(block):
        return block.astype(jnp.float32)

    def core(h, half, q):
        owner = far if half == 0 else mate
        return remote(
            x_ref.at[h, owner * SIDE + q], core_in.at[h, half * SIDE + q],
            core_s.at[h, half * SIDE + q], core_r.at[h, half * SIDE + q], {"expert": mate},
        )

    def over(h, q):
        return remote(
            over_out.at[h, q], over_in.at[h, q], over_s.at[h, q], over_r.at[h, q],
            {"expert": across},
        )

    def up(h, q):
        return remote(
            chain_out.at[h, q], up_in.at[h, q], up_s.at[h, q], up_r.at[h, q], {"dp": z + 1}
        )

    def down(h, q):
        return remote(
            chain_out.at[h, q], down_in.at[h, q], down_s.at[h, q], down_r.at[h, q],
            {"dp": z - 1},
        )

    def steps(places):
        return [(q, h) for q in places for h in range(CHUNKS)]

    for half in range(2):
        for q, h in steps(order):
            core(h, half, q).start()
    for q, h in steps(order):
        core(h, 0, q).wait_recv()
        both = f32(x_ref[h, across * SIDE + q]) + f32(core_in[h, q])
        over_out[h, q] = both.astype(jnp.bfloat16)
        over(h, q).start()

    def here(h, q):
        core(h, 1, q).wait_recv()
        over(h, q).wait_recv()
        return f32(x_ref[h, e * SIDE + q]) + f32(core_in[h, SIDE + q]) + f32(over_in[h, q])

    for q, h in steps(order[:-1]):
        both = here(h, q)

        @pl.when(((q > z) & (z == 0)) | ((q < z) & (z == SIDE - 1)))
        def _():
            chain_out[h, q] = both.astype(jnp.bfloat16)

        @pl.when((q > z) & (z > 0))
        def _():
            up(h, q).wait_recv()
            chain_out[h, q] = (both + f32(up_in[h, q])).astype(jnp.bfloat16)

        @pl.when((q < z) & (z < SIDE - 1))
        def _():
            down(h, q).wait_recv()
            chain_out[h, q] = (both + f32(down_in[h, q])).astype(jnp.bfloat16)

        @pl.when(q > z)
        def _():
            up(h, q).start()

        @pl.when(q < z)
        def _():
            down(h, q).start()

    for h in range(CHUNKS):
        total = here(h, z)

        @pl.when(z == 0)
        def _():
            down(h, z).wait_recv()
            out_ref[h] = (total + f32(down_in[h, z])).astype(jnp.bfloat16)

        @pl.when(z == SIDE - 1)
        def _():
            up(h, z).wait_recv()
            out_ref[h] = (total + f32(up_in[h, z])).astype(jnp.bfloat16)

        @pl.when((z > 0) & (z < SIDE - 1))
        def _():
            up(h, z).wait_recv()
            down(h, z).wait_recv()
            out_ref[h] = (total + f32(up_in[h, z]) + f32(down_in[h, z])).astype(jnp.bfloat16)

    for half in range(2):
        for q, h in steps(order):
            core(h, half, q).wait_send()
    for q, h in steps(order):
        over(h, q).wait_send()
    for q, h in steps(order[:-1]):

        @pl.when(q > z)
        def _():
            up(h, q).wait_send()

        @pl.when(q < z)
        def _():
            down(h, q).wait_send()


def square_group():
    return lax.axis_size("expert") == SIDE and lax.axis_size("dp") == SIDE


def gather(block):
    flat = block.reshape(-1, block.shape[-1])
    if not square_group():
        return lax.all_gather(flat, GROUP, axis=0, tiled=True)
    slots = SIDE * SIDE
    width = flat.shape[-1]
    chunk = flat.shape[0] // CHUNKS
    got = pl.pallas_call(
        gather_kernel,
        out_shape=jax.ShapeDtypeStruct((CHUNKS, slots, chunk, width), flat.dtype),
        in_specs=[pl.BlockSpec(memory_space=pl.ANY)],
        out_specs=pl.BlockSpec(memory_space=pl.ANY),
        scratch_shapes=[
            pltpu.SemaphoreType.DMA((CHUNKS,)),
            pltpu.SemaphoreType.DMA((CHUNKS, slots, 4)),
            pltpu.SemaphoreType.DMA((CHUNKS, slots)),
        ],
        compiler_params=pltpu.CompilerParams(collective_id=0, has_side_effects=True),
    )(flat.reshape(CHUNKS, chunk, width))
    return got.reshape(-1, width)


def scatter_sum(partial, like):
    if not square_group():
        summed = lax.psum_scatter(partial, GROUP, scatter_dimension=0, tiled=True)
        return summed.reshape(like.shape)
    width = partial.shape[-1]
    rows = partial.shape[0] // (SIDE * SIDE * CHUNKS)
    buffers = [pltpu.VMEM((CHUNKS, n, rows, width), partial.dtype) for n in (8, 4, 4, 4, 4, 4)]
    sems = [pltpu.SemaphoreType.DMA((CHUNKS, n)) for n in (8, 8, 4, 4, 4, 4, 4, 4)]
    summed = pl.pallas_call(
        scatter_kernel,
        out_shape=jax.ShapeDtypeStruct((CHUNKS, rows, width), partial.dtype),
        in_specs=[pl.BlockSpec(memory_space=pltpu.VMEM)],
        out_specs=pl.BlockSpec(memory_space=pltpu.VMEM),
        scratch_shapes=buffers + sems,
        compiler_params=pltpu.CompilerParams(
            collective_id=1, has_side_effects=True, vmem_limit_bytes=32 * 1024 * 1024
        ),
    )(partial.reshape(CHUNKS, SIDE * SIDE, rows, width))
    return summed.reshape(like.shape)


def mm(a, b, dims=((1,), (0,))):
    return lax.dot_general(a, b, (dims, ((), ())), preferred_element_type=jnp.float32)


def shards(inputs, upstream, route_mask, route_weights, gate_weight, up_weight, down_weight):
    sections = lax.axis_size("section")
    section = lax.axis_index("section")
    gate_w, up_w, down_w = gate_weight[0], up_weight[0], down_weight[0]
    mask = route_mask[0]
    table = slot_tables(mask)
    weights = jnp.sum(table.astype(jnp.float32) * route_weights[0][:, :, None], axis=1)[:, :, None]
    up_route = [(i, i + 1) for i in range(sections - 1)]
    down_route = [(i + 1, i) for i in range(sections - 1)]
    next_table = lax.ppermute(table, "section", down_route)
    previous_table = lax.ppermute(table, "section", up_route)

    def activations(gate_pre, up_pre):
        return (jax.nn.silu(gate_pre) * up_pre).astype(jnp.bfloat16)

    def out_grad(g_rows):
        return (weights * g_rows.astype(jnp.float32)).astype(jnp.bfloat16)

    stream = inputs
    current = pick(table, inputs)
    last_rows = pick(table, upstream)
    grads_in = last_rows
    first_grad = out_grad(last_rows)
    is_last = section == sections - 1
    own = current
    all_rows = gate_pre = up_pre = all_grads = hidden_grad = None
    for t in range(sections):
        active = section == t
        own = jnp.where(active, current, own)
        own_f = current.astype(jnp.float32)
        normed = (own_f * row_scale(own_f)).astype(jnp.bfloat16)
        send = jnp.where(is_last, first_grad, normed) if t == 0 and sections > 1 else normed
        got = gather(send)
        if t == 0:
            all_grads = got if sections > 1 else gather(first_grad)
            hidden_grad = mm(all_grads, down_w, ((1,), (1,)))
            all_rows = got
            gate_pre = mm(got, gate_w)
            up_pre = mm(got, up_w)
            new_gate, new_up = gate_pre, up_pre
        else:
            new_gate, new_up = mm(got, gate_w), mm(got, up_w)
            all_rows = jnp.where(active, got, all_rows)
            gate_pre = jnp.where(active, new_gate, gate_pre)
            up_pre = jnp.where(active, new_up, up_pre)
        if t < sections - 1:
            partial = mm(activations(new_gate, new_up), down_w).astype(jnp.bfloat16)
            back = scatter_sum(partial, current).astype(jnp.float32)
            output_rows = (own_f + weights * back).astype(jnp.bfloat16)
            output = place(table, mask, output_rows, stream)
            if t == sections - 2:
                current = lax.ppermute(pick(next_table, output), "section", up_route)
            else:
                stream = lax.ppermute(output, "section", up_route)
                current = pick(table, stream)

    sigma = jax.nn.sigmoid(gate_pre)
    silu_val = jax.nn.silu(gate_pre)
    hidden = activations(gate_pre, up_pre)
    slope = up_pre * sigma * (1.0 + gate_pre * (1.0 - sigma))
    own_f = own.astype(jnp.float32)
    scale = row_scale(own_f)

    flow = upstream
    for t in reversed(range(sections)):
        active = section == t
        if t < sections - 1:
            got = gather(out_grad(grads_in))
            all_grads = jnp.where(active, got, all_grads)
            hidden_grad = mm(all_grads, down_w, ((1,), (1,)))
        gate_units = (hidden_grad * slope).astype(jnp.bfloat16)
        up_units = (hidden_grad * silu_val).astype(jnp.bfloat16)
        if t > 0:
            partial = mm(gate_units, gate_w, ((1,), (1,))) + mm(up_units, up_w, ((1,), (1,)))
            total = scatter_sum(partial.astype(jnp.bfloat16), own).astype(jnp.float32)
            inner = jnp.mean(own_f * total, axis=-1, keepdims=True)
            grad_rows = (
                grads_in.astype(jnp.float32)
                + scale * total
                - own_f * (scale * scale * scale) * inner
            ).astype(jnp.bfloat16)
            result = place(table, mask, grad_rows, flow)
            if t == 1:
                grads_in = lax.ppermute(pick(previous_table, result), "section", down_route)
            else:
                flow = lax.ppermute(result, "section", down_route)
                grads_in = pick(table, flow)

    gate_grad = mm(all_rows, gate_units, ((0,), (0,)))
    up_grad = mm(all_rows, up_units, ((0,), (0,)))
    down_grad = mm(hidden, all_grads, ((0,), (0,)))
    return (
        gate_grad.astype(jnp.bfloat16)[None],
        up_grad.astype(jnp.bfloat16)[None],
        down_grad.astype(jnp.bfloat16)[None],
    )


def solution(mesh):
    return jax.shard_map(
        shards,
        mesh=mesh,
        in_specs=(
            P(None, ("expert", "dp"), None),
            P(None, ("expert", "dp"), None),
            P("section", None, ("expert", "dp")),
            P("section", None, ("expert", "dp")),
            P("section", None, ("expert", "dp")),
            P("section", None, ("expert", "dp")),
            P("section", ("expert", "dp"), None),
        ),
        out_specs=(
            P("section", None, ("expert", "dp")),
            P("section", None, ("expert", "dp")),
            P("section", ("expert", "dp"), None),
        ),
        check_vma=False,
    )
```

```python
import jax
import jax.numpy as jnp
from jax import lax
from jax.experimental import pallas as pl
from jax.experimental.pallas import tpu as pltpu
from jax.sharding import PartitionSpec as P

CAP = 8

EPSILON = 1e-05

GROUP = ("expert", "dp")


def slot_tables(mask):
    position = jnp.cumsum(mask, axis=1) - 1
    chosen = (mask[:, :, None] == 1) & (
        position[:, :, None] == jnp.arange(CAP, dtype=jnp.int32)[None, None, :]
    )
    return chosen.astype(jnp.bfloat16)


def pick(table, values):
    return lax.dot_general(
        table, values, (((1,), (1,)), ((0,), (0,))), preferred_element_type=jnp.float32
    ).astype(values.dtype)


def place(table, mask, rows, values):
    spread = lax.dot_general(
        table, rows, (((2,), (1,)), ((0,), (0,))), preferred_element_type=jnp.float32
    ).astype(values.dtype)
    return jnp.where(mask[:, :, None] == 1, spread, values)


def row_scale(rows_f):
    return lax.rsqrt(jnp.mean(rows_f * rows_f, axis=-1, keepdims=True) + EPSILON)


SIDE = 4
CHUNKS = 2


def neighbours():
    e, z = lax.axis_index("expert"), lax.axis_index("dp")
    mate = e + 1 - 2 * lax.rem(e, 2)
    across = lax.rem(e + 2, SIDE)
    return e, z, mate, across


def remote(src, dst, send_sem, recv_sem, target):
    return pltpu.make_async_remote_copy(
        src_ref=src,
        dst_ref=dst,
        send_sem=send_sem,
        recv_sem=recv_sem,
        device_id=target,
        device_id_type=pl.DeviceIdType.MESH,
    )


def entry_barrier(z, mate, across):
    barrier = pltpu.get_barrier_semaphore()

    def greet(target):
        pl.semaphore_signal(
            barrier, inc=1, device_id=target, device_id_type=pl.DeviceIdType.MESH
        )

    greet({"expert": mate})
    greet({"expert": across})

    @pl.when(z > 0)
    def _():
        greet({"dp": z - 1})

    @pl.when(z < SIDE - 1)
    def _():
        greet({"dp": z + 1})

    @pl.when((z > 0) & (z < SIDE - 1))
    def _():
        pl.semaphore_wait(barrier, 4)

    @pl.when((z == 0) | (z == SIDE - 1))
    def _():
        pl.semaphore_wait(barrier, 3)


def gather_kernel(x_ref, out_ref, local_sem, send_sem, recv_sem):
    e, z, mate, across = neighbours()
    entry_barrier(z, mate, across)

    def route(h, slot, kind, target, mine=False):
        block = x_ref.at[h] if mine else out_ref.at[h, slot]
        return remote(
            block, out_ref.at[h, slot], send_sem.at[h, slot, kind], recv_sem.at[h, slot], target
        )

    def up(h, slot, mine=False):
        return route(h, slot, 0, {"dp": z + 1}, mine)

    def down(h, slot, mine=False):
        return route(h, slot, 1, {"dp": z - 1}, mine)

    def over(h, slot, mine=False):
        return route(h, slot, 2, {"expert": across}, mine)

    def core(h, slot, mine=False):
        return route(h, slot, 3, {"expert": mate}, mine)

    own = e * SIDE + z

    def own_sends(act):
        for h in range(CHUNKS):

            @pl.when(z < SIDE - 1)
            def _():
                act(up(h, own, True))

            @pl.when(z > 0)
            def _():
                act(down(h, own, True))

            act(over(h, own, True))
            act(core(h, own, True))

    def keep(h):
        return pltpu.make_async_copy(x_ref.at[h], out_ref.at[h, own], local_sem.at[h])

    own_sends(lambda copy: copy.start())
    for h in range(CHUNKS):
        keep(h).start()

    def chain(act, arrive):
        for d in range(1, SIDE):
            for h in range(CHUNKS):

                @pl.when(z - d >= 0)
                def _():
                    slot = e * SIDE + z - d
                    if arrive:
                        core(h, slot).wait_recv()

                    @pl.when(z < SIDE - 1)
                    def _():
                        act(up(h, slot))

                    act(over(h, slot))
                    act(core(h, slot))

                @pl.when(z + d < SIDE)
                def _():
                    slot = e * SIDE + z + d
                    if arrive:
                        core(h, slot).wait_recv()

                    @pl.when(z > 0)
                    def _():
                        act(down(h, slot))

                    act(over(h, slot))
                    act(core(h, slot))

    chain(lambda copy: copy.start(), True)
    for d in range(SIDE):
        for h in range(CHUNKS):
            slot = across * SIDE + lax.rem(z + d, SIDE)
            core(h, slot).wait_recv()
            core(h, slot).start()
    far = lax.rem(mate + 2, SIDE)
    for h in range(CHUNKS):
        for d in range(SIDE):
            core(h, mate * SIDE + lax.rem(z + d, SIDE)).wait_recv()
            core(h, far * SIDE + lax.rem(z + d, SIDE)).wait_recv()
    own_sends(lambda copy: copy.wait_send())
    for h in range(CHUNKS):
        keep(h).wait()
    chain(lambda copy: copy.wait_send(), False)
    for h in range(CHUNKS):
        for d in range(SIDE):
            core(h, across * SIDE + lax.rem(z + d, SIDE)).wait_send()


def scatter_kernel(
    x_ref, out_ref, core_in, over_in, up_in, down_in, over_out, chain_out,
    core_s, core_r, over_s, over_r, up_s, up_r, down_s, down_r,
):
    e, z, mate, across = neighbours()
    far = lax.rem(mate + 2, SIDE)
    entry_barrier(z, mate, across)
    order = [lax.rem(z + d, SIDE) for d in (2, 3, 1, 0)]

    def f32(block):
        return block.astype(jnp.float32)

    def core(h, half, q):
        owner = far if half == 0 else mate
        return remote(
            x_ref.at[h, owner * SIDE + q], core_in.at[h, half * SIDE + q],
            core_s.at[h, half * SIDE + q], core_r.at[h, half * SIDE + q], {"expert": mate},
        )

    def over(h, q):
        return remote(
            over_out.at[h, q], over_in.at[h, q], over_s.at[h, q], over_r.at[h, q],
            {"expert": across},
        )

    def up(h, q):
        return remote(
            chain_out.at[h, q], up_in.at[h, q], up_s.at[h, q], up_r.at[h, q], {"dp": z + 1}
        )

    def down(h, q):
        return remote(
            chain_out.at[h, q], down_in.at[h, q], down_s.at[h, q], down_r.at[h, q],
            {"dp": z - 1},
        )

    def steps(places):
        return [(q, h) for q in places for h in range(CHUNKS)]

    for half in range(2):
        for q, h in steps(order):
            core(h, half, q).start()
    for q, h in steps(order):
        core(h, 0, q).wait_recv()
        both = f32(x_ref[h, across * SIDE + q]) + f32(core_in[h, q])
        over_out[h, q] = both.astype(jnp.bfloat16)
        over(h, q).start()

    def here(h, q):
        core(h, 1, q).wait_recv()
        over(h, q).wait_recv()
        return f32(x_ref[h, e * SIDE + q]) + f32(core_in[h, SIDE + q]) + f32(over_in[h, q])

    for q, h in steps(order[:-1]):
        both = here(h, q)

        @pl.when(((q > z) & (z == 0)) | ((q < z) & (z == SIDE - 1)))
        def _():
            chain_out[h, q] = both.astype(jnp.bfloat16)

        @pl.when((q > z) & (z > 0))
        def _():
            up(h, q).wait_recv()
            chain_out[h, q] = (both + f32(up_in[h, q])).astype(jnp.bfloat16)

        @pl.when((q < z) & (z < SIDE - 1))
        def _():
            down(h, q).wait_recv()
            chain_out[h, q] = (both + f32(down_in[h, q])).astype(jnp.bfloat16)

        @pl.when(q > z)
        def _():
            up(h, q).start()

        @pl.when(q < z)
        def _():
            down(h, q).start()

    for h in range(CHUNKS):
        total = here(h, z)

        @pl.when(z == 0)
        def _():
            down(h, z).wait_recv()
            out_ref[h] = (total + f32(down_in[h, z])).astype(jnp.bfloat16)

        @pl.when(z == SIDE - 1)
        def _():
            up(h, z).wait_recv()
            out_ref[h] = (total + f32(up_in[h, z])).astype(jnp.bfloat16)

        @pl.when((z > 0) & (z < SIDE - 1))
        def _():
            up(h, z).wait_recv()
            down(h, z).wait_recv()
            out_ref[h] = (total + f32(up_in[h, z]) + f32(down_in[h, z])).astype(jnp.bfloat16)

    for half in range(2):
        for q, h in steps(order):
            core(h, half, q).wait_send()
    for q, h in steps(order):
        over(h, q).wait_send()
    for q, h in steps(order[:-1]):

        @pl.when(q > z)
        def _():
            up(h, q).wait_send()

        @pl.when(q < z)
        def _():
            down(h, q).wait_send()


def square_group():
    return lax.axis_size("expert") == SIDE and lax.axis_size("dp") == SIDE


def gather(block):
    flat = block.reshape(-1, block.shape[-1])
    if not square_group():
        return lax.all_gather(flat, GROUP, axis=0, tiled=True)
    slots = SIDE * SIDE
    width = flat.shape[-1]
    chunk = flat.shape[0] // CHUNKS
    got = pl.pallas_call(
        gather_kernel,
        out_shape=jax.ShapeDtypeStruct((CHUNKS, slots, chunk, width), flat.dtype),
        in_specs=[pl.BlockSpec(memory_space=pl.ANY)],
        out_specs=pl.BlockSpec(memory_space=pl.ANY),
        scratch_shapes=[
            pltpu.SemaphoreType.DMA((CHUNKS,)),
            pltpu.SemaphoreType.DMA((CHUNKS, slots, 4)),
            pltpu.SemaphoreType.DMA((CHUNKS, slots)),
        ],
        compiler_params=pltpu.CompilerParams(
            collective_id=0, has_side_effects=True, vmem_limit_bytes=1024 * 1024
        ),
    )(flat.reshape(CHUNKS, chunk, width))
    return got.reshape(-1, width)


def scatter_sum(partial, like):
    if not square_group():
        summed = lax.psum_scatter(partial, GROUP, scatter_dimension=0, tiled=True)
        return summed.reshape(like.shape)
    width = partial.shape[-1]
    rows = partial.shape[0] // (SIDE * SIDE * CHUNKS)
    buffers = [pltpu.VMEM((CHUNKS, n, rows, width), partial.dtype) for n in (8, 4, 4, 4, 4, 4)]
    sems = [pltpu.SemaphoreType.DMA((CHUNKS, n)) for n in (8, 8, 4, 4, 4, 4, 4, 4)]
    summed = pl.pallas_call(
        scatter_kernel,
        out_shape=jax.ShapeDtypeStruct((CHUNKS, rows, width), partial.dtype),
        in_specs=[pl.BlockSpec(memory_space=pltpu.VMEM)],
        out_specs=pl.BlockSpec(memory_space=pltpu.VMEM),
        scratch_shapes=buffers + sems,
        compiler_params=pltpu.CompilerParams(
            collective_id=1, has_side_effects=True, vmem_limit_bytes=16 * 1024 * 1024
        ),
    )(partial.reshape(CHUNKS, SIDE * SIDE, rows, width))
    return summed.reshape(like.shape)


def mm(a, b, dims=((1,), (0,))):
    return lax.dot_general(a, b, (dims, ((), ())), preferred_element_type=jnp.float32)


def shards(inputs, upstream, route_mask, route_weights, gate_weight, up_weight, down_weight):
    sections = lax.axis_size("section")
    section = lax.axis_index("section")
    gate_w, up_w, down_w = gate_weight[0], up_weight[0], down_weight[0]
    mask = route_mask[0]
    table = slot_tables(mask)
    weights = jnp.sum(table.astype(jnp.float32) * route_weights[0][:, :, None], axis=1)[:, :, None]
    up_route = [(i, i + 1) for i in range(sections - 1)]
    down_route = [(i + 1, i) for i in range(sections - 1)]
    next_table = lax.ppermute(table, "section", down_route)
    previous_table = lax.ppermute(table, "section", up_route)

    def activations(gate_pre, up_pre):
        return (jax.nn.silu(gate_pre) * up_pre).astype(jnp.bfloat16)

    def out_grad(g_rows):
        return (weights * g_rows.astype(jnp.float32)).astype(jnp.bfloat16)

    stream = inputs
    current = pick(table, inputs)
    last_rows = pick(table, upstream)
    grads_in = last_rows
    first_grad = out_grad(last_rows)
    is_last = section == sections - 1
    own = current
    all_rows = gate_pre = up_pre = all_grads = None
    for t in range(sections):
        active = section == t
        own = jnp.where(active, current, own)
        own_f = own.astype(jnp.float32)
        normed = (own_f * row_scale(own_f)).astype(jnp.bfloat16)
        send = jnp.where(is_last, first_grad, normed) if t == 0 and sections > 1 else normed
        got = gather(send)
        if t == 0:
            all_grads = got if sections > 1 else gather(first_grad)
        all_rows = got
        gate_pre, up_pre = mm(got, gate_w), mm(got, up_w)
        if t < sections - 1:
            partial = mm(activations(gate_pre, up_pre), down_w).astype(jnp.bfloat16)
            back = scatter_sum(partial, own).astype(jnp.float32)
            output_rows = (own_f + weights * back).astype(jnp.bfloat16)
            output = place(table, mask, output_rows, stream)
            if t == sections - 2:
                current = lax.ppermute(pick(next_table, output), "section", up_route)
            else:
                stream = lax.ppermute(output, "section", up_route)
                current = pick(table, stream)

    sigma = jax.nn.sigmoid(gate_pre)
    silu_val = jax.nn.silu(gate_pre)
    hidden = activations(gate_pre, up_pre)
    slope = up_pre * sigma * (1.0 + gate_pre * (1.0 - sigma))
    own_f = own.astype(jnp.float32)
    scale = row_scale(own_f)

    flow = upstream
    own_grad = first_grad
    all_grads, all_rows = lax.optimization_barrier((all_grads, all_rows))
    for t in reversed(range(sections)):
        active = section == t
        if t < sections - 1:
            own_grad = jnp.where(active, out_grad(grads_in), own_grad)
            all_grads = gather(own_grad)
        hidden_grad = mm(all_grads, down_w, ((1,), (1,)))
        gate_units = (hidden_grad * slope).astype(jnp.bfloat16)
        up_units = (hidden_grad * silu_val).astype(jnp.bfloat16)
        if t > 0:
            partial = mm(gate_units, gate_w, ((1,), (1,))) + mm(up_units, up_w, ((1,), (1,)))
            total = scatter_sum(partial.astype(jnp.bfloat16), own).astype(jnp.float32)
            inner = jnp.mean(own_f * total, axis=-1, keepdims=True)
            grad_rows = (
                grads_in.astype(jnp.float32)
                + scale * total
                - own_f * (scale * scale * scale) * inner
            ).astype(jnp.bfloat16)
            result = place(table, mask, grad_rows, flow)
            if t == 1:
                grads_in = lax.ppermute(pick(previous_table, result), "section", down_route)
            else:
                flow = lax.ppermute(result, "section", down_route)
                grads_in = pick(table, flow)

    gate_grad = mm(all_rows, gate_units, ((0,), (0,)))
    up_grad = mm(all_rows, up_units, ((0,), (0,)))
    down_grad = mm(hidden, all_grads, ((0,), (0,)))
    return (
        gate_grad.astype(jnp.bfloat16)[None],
        up_grad.astype(jnp.bfloat16)[None],
        down_grad.astype(jnp.bfloat16)[None],
    )


def solution(mesh):
    return jax.shard_map(
        shards,
        mesh=mesh,
        in_specs=(
            P(None, ("expert", "dp"), None),
            P(None, ("expert", "dp"), None),
            P("section", None, ("expert", "dp")),
            P("section", None, ("expert", "dp")),
            P("section", None, ("expert", "dp")),
            P("section", None, ("expert", "dp")),
            P("section", ("expert", "dp"), None),
        ),
        out_specs=(
            P("section", None, ("expert", "dp")),
            P("section", None, ("expert", "dp")),
            P("section", ("expert", "dp"), None),
        ),
        check_vma=False,
    )
```
